32 devices in a mesh: clip: 1, head: 16 (over z, y, x), kv: 2 (over core).
Axes of the slice: x: 2, y: 2, z: 4, core: 2. Of those that a mesh axis runs over, the one named last changes fastest.
Arguments:
- queries: bfloat16 [4096, 4096], P(('clip', 'head')), may hold values from -7 to 7
- keys: bfloat16 [8192, 4096], P(('clip', 'head', 'kv')), may hold values from -5 to 5
- values: bfloat16 [8192, 4096], P(('clip', 'head', 'kv')), may hold values from -6 to 6
- tile_list: int32 [32, 32], P('clip'), may hold values from 0 to 63, as said below
Outputs:
- attended: bfloat16 [4096, 4096], P(('clip', 'head', 'kv'))
The draws below stay inside these ranges and needn't reach their ends.
Inputs may be any that keep to these rules, and one draw needn't show every extreme that they name: `tile_list`: each row names 32 different key tiles. Calling a tile t even when (t // 2) is even, a row names at most 20 even tiles and at most 20 others; some row names exactly 20 even tiles and some row exactly 20 others, in every draw.
All inputs are finite; a program needn't handle non-finite values.
Results may differ from the reference program's by a relative error of at most 0.014.
Values may be sent and summed in bfloat16 or wider, within the bound.
No kernel may reach another device: no remote copies, remote signals or barrier semaphores. Data moves between devices by JAX's collectives and lax.ppermute only.
A program may use at most 128 MiB of HBM per device.

```python
import jax
import jax.numpy as jnp
from jax import lax

HEADS = 32
DH = 128
TILE = 128
NSEL = 32
LMAX = 20
KTOK_DEV = 256
SQ = 4096
SK = 8192
QTILES = 32
KTILES = 64


def spike_signs(key):
    coins = jax.random.bernoulli(jax.random.fold_in(key, 91), 0.5, (HEADS * DH,))
    return jnp.where(coins, 1.0, -1.0).astype(jnp.float32)


def draw_queries(key, part):
    base_key = jax.random.fold_in(key, 1)
    drawn = jnp.clip(jax.random.normal(base_key, (SQ, HEADS * DH), jnp.float32), -5.0, 5.0)
    token_pos = jnp.arange(SQ)
    widen = jnp.sqrt(jnp.float32(128.0) / jnp.float32(DH))
    strength = (3.0 + 2.0 * (token_pos // TILE % 3)).astype(jnp.float32) * widen
    spiked = strength[:, None] * spike_signs(key)[None, :]
    return jnp.where((token_pos % TILE == 0)[:, None], spiked, drawn).astype(jnp.bfloat16)


def draw_keys(key, part):
    base_key = jax.random.fold_in(key, 2)
    drawn = jnp.clip(jax.random.normal(base_key, (SK, HEADS * DH), jnp.float32), -5.0, 5.0)
    token_pos = jnp.arange(SK)
    signs = spike_signs(key)[None, :]
    drawn = jnp.where((token_pos % TILE == 0)[:, None], 3.0 * signs, drawn)
    return jnp.where((token_pos % TILE == 1)[:, None], 2.96875 * signs, drawn).astype(jnp.bfloat16)


def draw_tile_list(key, part):
    key_one, key_two, key_three = jax.random.split(key, 3)
    query_pos = jnp.arange(QTILES, dtype=jnp.int32)
    key_pos = jnp.arange(KTILES, dtype=jnp.int32)
    center = (KTILES - QTILES) // 2 + query_pos
    distance = jnp.abs(key_pos[None, :] - center[:, None])
    noise = jax.random.randint(key_one, (QTILES, KTILES), 0, 2 ** 20)
    priority = noise // (1 + distance) * KTILES + key_pos[None, :]
    parity = key_pos // (KTOK_DEV // TILE) % 2
    even_score = jnp.where(parity[None, :] == 0, priority, -1)
    odd_score = jnp.where(parity[None, :] == 1, priority, -1)
    even_top = jax.lax.top_k(even_score, KTILES // 2)[1].astype(jnp.int32)
    odd_top = jax.lax.top_k(odd_score, KTILES // 2)[1].astype(jnp.int32)
    even_count = jax.random.randint(key_two, (QTILES,), NSEL - LMAX, LMAX + 1)
    picked = jax.random.permutation(key_three, QTILES)
    even_count = even_count.at[picked[0]].set(LMAX).at[picked[1]].set(NSEL - LMAX)
    slot_pos = jnp.arange(NSEL, dtype=jnp.int32)[None, :]
    from_even = slot_pos < even_count[:, None]
    even_pick = jnp.take_along_axis(even_top, jnp.broadcast_to(slot_pos, (QTILES, NSEL)), axis=1)
    odd_slot = jnp.clip(slot_pos - even_count[:, None], 0, NSEL - 1)
    odd_pick = jnp.take_along_axis(odd_top, odd_slot, axis=1)
    return jnp.where(from_even, even_pick, odd_pick).astype(jnp.int32)


def steps_of(own_key, extent, shards, low, high):
    gain, own = 1.0, jax.random.fold_in(own_key, 6)
    for dim, shards_of in shards:
        steps = jnp.exp(jax.random.uniform(jax.random.fold_in(own, dim), (shards_of,), jnp.float32, low / len(shards), high / len(shards)))
        gain = gain * jnp.repeat(steps, extent[dim] // shards_of).reshape([-1 if axis == dim else 1 for axis in range(len(extent))])
    return gain


def bell_draw(rng, dims, scale, limit, pieces=(), held_as=jnp.bfloat16):
    factor_of = steps_of(rng, dims, pieces, -0.22, 0.18) if pieces else 1.0
    values = jax.random.normal(rng, dims, jnp.float32) * scale * factor_of
    return jnp.minimum(jnp.maximum(values, -limit), limit).astype(held_as)


def setup_inputs(seed: int = 0, part: int = 0) -> dict:
    arg_keys = jax.random.split(jax.random.key(seed), 5)
    part_keys = jax.random.split(jax.random.fold_in(arg_keys[4], part), 5)
    queries = draw_queries(jax.random.fold_in(jax.random.fold_in(arg_keys[4], part), 71), part)
    keys = draw_keys(jax.random.fold_in(jax.random.fold_in(arg_keys[4], part), 71), part)
    values = bell_draw(part_keys[2], (SK, HEADS * DH), 1.0, 6.0, ((0, 32),))
    tile_list = draw_tile_list(jax.random.fold_in(jax.random.fold_in(arg_keys[4], part), 71), part)
    return {"queries": queries, "keys": keys, "values": values, "tile_list": tile_list}


def reference(queries, keys, values, tile_list):
    inv_root = 1.0 / jnp.sqrt(jnp.float32(DH))
    key_tiles = keys.reshape(KTILES, TILE, HEADS, DH)
    value_tiles = values.reshape(KTILES, TILE, HEADS, DH)

    def one_tile(tile_index):
        query_rows = lax.dynamic_slice_in_dim(queries, tile_index * TILE, TILE, 0)
        query_rows = query_rows.reshape(TILE, HEADS, DH).astype(jnp.float32)
        chosen = tile_list[tile_index]
        key_block = key_tiles[chosen].reshape(NSEL * TILE, HEADS, DH).astype(jnp.float32)
        value_block = value_tiles[chosen].reshape(NSEL * TILE, HEADS, DH).astype(jnp.float32)
        scores = jnp.einsum('qhd,khd->hqk', query_rows, key_block) * inv_root
        row_peak = lax.optimization_barrier(jnp.max(scores, axis=-1, keepdims=True))
        exponent = jnp.exp(scores - row_peak)
        row_total = lax.optimization_barrier(jnp.sum(exponent, axis=-1))
        weight = lax.optimization_barrier(exponent.astype(jnp.bfloat16)).astype(jnp.float32)
        weighted = jnp.einsum('hqk,khd->qhd', weight, value_block)
        result = weighted / row_total.T[:, :, None]
        return result.reshape(TILE, HEADS * DH).astype(jnp.bfloat16)
    result_tiles = lax.map(one_tile, jnp.arange(QTILES, dtype=jnp.int32))
    return result_tiles.reshape(SQ, HEADS * DH)
```

```python
import functools
import math

import jax
import jax.numpy as jnp
from jax import lax
from jax.experimental import pallas as pl
from jax.experimental.pallas import tpu as pltpu
from jax.sharding import PartitionSpec as P

HEADS = 32
DH = 128
TILE = 128
CHUNK = 4
GROUPS = 2
LOW = -1e30


def block_kernel(q_ref, k_ref, v_ref, qo_ref, ko_ref, vo_ref):
    qo_ref[0] = q_ref[...]
    ko_ref[0] = k_ref[...]
    vo_ref[0] = v_ref[...]


def split_columns(kv_index, queries, keys, values, parts):
    half_rows = queries.shape[0] // 2
    width = queries.shape[1] // parts
    k_rows = keys.shape[0]
    grid_spec = pltpu.PrefetchScalarGridSpec(
        num_scalar_prefetch=1,
        grid=(parts,),
        in_specs=[
            pl.BlockSpec((half_rows, width), lambda j, c: (c[0], j)),
            pl.BlockSpec((k_rows, width), lambda j, c: (0, j)),
            pl.BlockSpec((k_rows, width), lambda j, c: (0, j)),
        ],
        out_specs=[
            pl.BlockSpec((1, half_rows, width), lambda j, c: (j, 0, 0)),
            pl.BlockSpec((1, k_rows, width), lambda j, c: (j, 0, 0)),
            pl.BlockSpec((1, k_rows, width), lambda j, c: (j, 0, 0)),
        ],
    )

    def body(c_ref, *refs):
        block_kernel(*refs)

    return pl.pallas_call(
        body,
        grid_spec=grid_spec,
        out_shape=[
            jax.ShapeDtypeStruct((parts, half_rows, width), queries.dtype),
            jax.ShapeDtypeStruct((parts, k_rows, width), keys.dtype),
            jax.ShapeDtypeStruct((parts, k_rows, width), values.dtype),
        ],
        name="split_columns",
    )(kv_index.reshape(1), queries, keys, values)


def attend_kernel(
    heads, tiles_src, lists_ref, counts_ref, q_ref, k0, k1, v0, v1, o_ref, st_ref,
    k_scr, v_scr, m_scr, l_scr, acc_scr, sems,
):
    unit = pl.program_id(0)

    @pl.when(unit == 0)
    def _():
        copies = [
            pltpu.make_async_copy(src, dst.at[pl.ds(base, tiles_src)], sems.at[n])
            for n, (src, dst, base) in enumerate(
                ((k0, k_scr, 0), (k1, k_scr, tiles_src), (v0, v_scr, 0), (v1, v_scr, tiles_src))
            )
        ]
        for copy in copies:
            copy.start()
        for copy in copies:
            copy.wait()

    scale = math.log2(math.e) / math.sqrt(DH)
    count = counts_ref[unit]
    m_scr[...] = jnp.full_like(m_scr, LOW)
    l_scr[...] = jnp.zeros_like(l_scr)
    acc_scr[...] = jnp.zeros_like(acc_scr)

    def step(first, masked):
        ids = [lists_ref[unit, first + n] for n in range(CHUNK)]
        for h in range(heads):
            cols = pl.ds(h * DH, DH)
            k_block = jnp.concatenate([k_scr[t, :, cols] for t in ids], axis=0)
            v_block = jnp.concatenate([v_scr[t, :, cols] for t in ids], axis=0)
            scores = lax.dot_general(
                q_ref[0, :, cols], k_block, (((1,), (1,)), ((), ())), preferred_element_type=jnp.float32
            )
            if masked:
                slot = first + lax.broadcasted_iota(jnp.int32, (1, CHUNK * TILE), 1) // TILE
                scores = jnp.where(slot < count, scores, LOW)
            m_old = m_scr[h]
            peak = jnp.max(scores, axis=1, keepdims=True)
            m_new = jnp.maximum(m_old, peak)
            m_scr[h] = m_new
            expo = jnp.exp2((scores - m_new[:, :1]) * scale)
            if masked:
                expo = jnp.where(slot < count, expo, 0.0)
            alpha = jnp.exp2((m_old - m_new) * scale)
            part = expo[:, :TILE]
            for n in range(1, CHUNK):
                part = part + expo[:, n * TILE : (n + 1) * TILE]
            l_scr[h] = l_scr[h] * alpha + part
            acc_scr[h] = acc_scr[h] * alpha + jnp.dot(
                expo.astype(jnp.bfloat16), v_block, preferred_element_type=jnp.float32
            )

    full = count // CHUNK

    def loop_body(i, carry):
        step(i * CHUNK, False)
        return carry

    lax.fori_loop(0, full, loop_body, 0)

    @pl.when(count % CHUNK != 0)
    def _():
        step(full * CHUNK, True)

    lane = lax.broadcasted_iota(jnp.int32, (TILE, TILE), 1)
    stats = jnp.full((TILE, TILE), LOW, jnp.float32)
    for h in range(heads):
        total = jnp.sum(l_scr[h], axis=1, keepdims=True)
        some = total > 0.0
        safe = jnp.where(some, total, 1.0)
        o_ref[0, :, pl.ds(h * DH, DH)] = (acc_scr[h] / safe).astype(o_ref.dtype)
        level = jnp.where(some, m_scr[h][:, :1] * scale + jnp.log2(safe), LOW)
        stats = jnp.where(lane == h, level, stats)
    st_ref[0] = stats.T[: st_ref.shape[1]]


def attend(lists, counts, q, k_pair, v_pair):
    units, rows, width = q.shape
    heads = width // DH
    stat_rows = -(-heads // 8) * 8
    as_tiles = lambda t: t.reshape(-1, TILE, width)
    k_pair = [as_tiles(t) for t in k_pair]
    v_pair = [as_tiles(t) for t in v_pair]
    tiles_src = k_pair[0].shape[0]
    anywhere = pl.BlockSpec(memory_space=pl.ANY)
    grid_spec = pltpu.PrefetchScalarGridSpec(
        num_scalar_prefetch=2,
        grid=(units,),
        in_specs=[pl.BlockSpec((1, rows, width), lambda u, *_: (u, 0, 0))] + [anywhere] * 4,
        out_specs=[
            pl.BlockSpec((1, rows, width), lambda u, *_: (u, 0, 0)),
            pl.BlockSpec((1, stat_rows, TILE), lambda u, *_: (u, 0, 0)),
        ],
        scratch_shapes=[
            pltpu.VMEM((2 * tiles_src, TILE, width), jnp.bfloat16),
            pltpu.VMEM((2 * tiles_src, TILE, width), jnp.bfloat16),
            pltpu.VMEM((heads, TILE, TILE), jnp.float32),
            pltpu.VMEM((heads, TILE, TILE), jnp.float32),
            pltpu.VMEM((heads, TILE, DH), jnp.float32),
            pltpu.SemaphoreType.DMA((4,)),
        ],
    )
    return pl.pallas_call(
        functools.partial(attend_kernel, heads, tiles_src),
        grid_spec=grid_spec,
        out_shape=[
            jax.ShapeDtypeStruct((units, rows, width), jnp.bfloat16),
            jax.ShapeDtypeStruct((units, stat_rows, TILE), jnp.float32),
        ],
        name="attend",
    )(lists, counts, q, *k_pair, *v_pair)


def merge_kernel(heads, oa_ref, sa_ref, ob_ref, sb_ref, o_ref):
    pad = jnp.zeros((TILE - sa_ref.shape[1], TILE), jnp.float32)
    level_a = jnp.concatenate([sa_ref[0], pad], axis=0).T
    level_b = jnp.concatenate([sb_ref[0], pad], axis=0).T
    top = jnp.maximum(level_a, level_b)
    weight_a = jnp.exp2(level_a - top)
    weight_b = jnp.exp2(level_b - top)
    total = weight_a + weight_b
    weight_a = weight_a / total
    weight_b = weight_b / total
    for h in range(heads):
        cols = pl.ds(h * DH, DH)
        merged = oa_ref[0, :, cols].astype(jnp.float32) * weight_a[:, h : h + 1]
        merged = merged + ob_ref[0, :, cols].astype(jnp.float32) * weight_b[:, h : h + 1]
        o_ref[0, :, cols] = merged.astype(o_ref.dtype)


def merge(oa, sa, ob, sb):
    units, rows, width = oa.shape
    stat_rows = sa.shape[1]
    o_spec = pl.BlockSpec((1, rows, width), lambda u: (u, 0, 0))
    s_spec = pl.BlockSpec((1, stat_rows, TILE), lambda u: (u, 0, 0))
    return pl.pallas_call(
        functools.partial(merge_kernel, width // DH),
        grid=(units,),
        in_specs=[o_spec, s_spec, o_spec, s_spec],
        out_specs=o_spec,
        out_shape=jax.ShapeDtypeStruct(oa.shape, oa.dtype),
        name="merge",
    )(oa, sa, ob, sb)


def join_kernel(x_ref, o_ref):
    o_ref[...] = x_ref[0]


def join_columns(x):
    parts, rows, width = x.shape
    return pl.pallas_call(
        join_kernel,
        grid=(parts,),
        in_specs=[pl.BlockSpec((1, rows, width), lambda j: (j, 0, 0))],
        out_specs=pl.BlockSpec((rows, width), lambda j: (0, j)),
        out_shape=jax.ShapeDtypeStruct((rows, parts * width), x.dtype),
        name="join_columns",
    )(x)


def key_lists(tile_list, span, group, kv_index, members):
    shard = tile_list // span
    owner = shard // 2
    inside = owner // members == group
    local = jnp.where(shard % 2 == kv_index, 0, members * span) + owner % members * span + tile_list % span
    slots = tile_list.shape[1]
    slot = jnp.arange(slots, dtype=jnp.int32)
    before = (slot[:, None] < slot[None, :]).astype(jnp.int32)
    flag = inside.astype(jnp.int32)
    place = jnp.sum(flag[:, :, None] * before[None], axis=1)
    hit = inside[:, :, None] & (place[:, :, None] == slot[None, None, :])
    packed = jnp.sum(jnp.where(hit, local[:, :, None], 0), axis=1)
    return packed, jnp.sum(flag, axis=1)


def local(queries, keys, values, tile_list):
    n_head = lax.axis_size("head")
    members = n_head // GROUPS
    kv_index = lax.axis_index("kv")
    head_index = lax.axis_index("head")
    group = head_index // members
    groups = [list(range(g * members, (g + 1) * members)) for g in range(GROUPS)]
    across = [(i, (i + members) % n_head) for i in range(n_head)]
    swap = [(0, 1), (1, 0)]

    exchange = functools.partial(
        lax.all_to_all, axis_name="head", split_axis=0, concat_axis=0, axis_index_groups=groups, tiled=True
    )
    q_blocks, k_blocks, v_blocks = split_columns(kv_index, queries, keys, values, members)
    q_own = exchange(q_blocks)
    q_far = lax.ppermute(q_own, "head", across)
    k_own = exchange(k_blocks)
    k_other = lax.ppermute(k_own, "kv", swap)
    v_own = exchange(v_blocks)
    v_other = lax.ppermute(v_own, "kv", swap)

    packed, number = key_lists(tile_list, keys.shape[0] // TILE, group, kv_index, members)
    units_src = queries.shape[0] // 2 // TILE
    packed = packed.reshape(GROUPS, members, 2, units_src, -1)
    number = number.reshape(GROUPS, members, 2, units_src)

    def lists_of(g):
        pick = lambda t: lax.dynamic_index_in_dim(
            lax.dynamic_index_in_dim(t, g, 0, False), kv_index, 1, False
        )
        return pick(packed).reshape(members * units_src, -1), pick(number).reshape(-1)

    width = q_own.shape[2]
    as_units = lambda t: t.reshape(members * units_src, TILE, width)
    lists, counts = lists_of(1 - group)
    o_far, s_far = attend(lists, counts, as_units(q_far), (k_own, k_other), (v_own, v_other))
    o_back = lax.ppermute(o_far, "head", across)
    s_back = lax.ppermute(s_far, "head", across)
    lists, counts = lists_of(group)
    o_near, s_near = attend(lists, counts, as_units(q_own), (k_own, k_other), (v_own, v_other))
    merged = merge(o_near, s_near, o_back, s_back).reshape(members, -1, width)
    return join_columns(exchange(merged))


def solution(mesh):
    return jax.shard_map(
        local,
        mesh=mesh,
        in_specs=(
            P(("clip", "head"), None),
            P(("clip", "head", "kv"), None),
            P(("clip", "head", "kv"), None),
            P("clip", None),
        ),
        out_specs=P(("clip", "head", "kv"), None),
        check_vma=False,
    )
```

```python
import functools
import math

import jax
import jax.numpy as jnp
from jax import lax
from jax.experimental import pallas as pl
from jax.experimental.pallas import tpu as pltpu
from jax.sharding import PartitionSpec as P


HEADS = 32
DH = 128
TILE = 128
STEP = 8
GROUPS = 2
LOW = -1e30
SCALE = math.log2(math.e) / math.sqrt(DH)


def split_queries(kv_index, queries, members, parts):
    rows = queries.shape[0] // 2
    width = queries.shape[1] // (members * parts)

    def body(c_ref, q_ref, *rest):
        outs, sems = rest[:parts], rest[parts]
        first = pl.multiple_of(c_ref[0] * rows, rows)
        copies = [
            pltpu.make_async_copy(
                q_ref.at[pl.ds(first, rows), pl.ds((j * parts + p) * width, width)], outs[p].at[j], sems.at[p, j]
            )
            for p in range(parts)
            for j in range(members)
        ]
        for copy in copies:
            copy.start()
        for copy in copies:
            copy.wait()

    anywhere = pl.BlockSpec(memory_space=pl.ANY)
    return pl.pallas_call(
        body,
        grid_spec=pltpu.PrefetchScalarGridSpec(
            num_scalar_prefetch=1,
            grid=(),
            in_specs=[anywhere],
            out_specs=[anywhere] * parts,
            scratch_shapes=[pltpu.SemaphoreType.DMA((parts, members))],
        ),
        out_shape=[jax.ShapeDtypeStruct((members, rows, width), queries.dtype)] * parts,
        name="split_queries",
    )(kv_index.reshape(1), queries)


def split_keys(keys, values, members, parts):
    rows, features = keys.shape
    tiles = rows // TILE
    heads = features // DH // (members * parts)
    group = math.gcd(members, 2)
    width = features // members * group

    def body(k_ref, v_ref, *outs):
        for g in range(group):
            for p in range(parts):
                for h in range(heads):
                    cols = pl.ds(((g * parts + p) * heads + h) * DH, DH)
                    for t in range(tiles):
                        outs[p][g, t, h] = k_ref[pl.ds(t * TILE, TILE), cols]
                        outs[p][g, t, heads + h] = v_ref[pl.ds(t * TILE, TILE), cols].T

    block = pl.BlockSpec((rows, width), lambda j: (0, j))
    return pl.pallas_call(
        body,
        grid=(members // group,),
        in_specs=[block, block],
        out_specs=[pl.BlockSpec((group, tiles, 2 * heads, TILE, DH), lambda j: (j, 0, 0, 0, 0))] * parts,
        out_shape=[jax.ShapeDtypeStruct((members, tiles, 2 * heads, TILE, DH), keys.dtype)] * parts,
        name="split_keys",
    )(keys, values)


def attend_kernel(
    heads, tiles_src, lists_ref, counts_ref, q_ref, near_ref, far_ref, o_ref, st_ref,
    kv_scr, m_scr, l_scr, acc_scr, sems,
):
    unit = pl.program_id(0)

    @pl.when(unit == 0)
    def _():
        copies = [
            pltpu.make_async_copy(src, kv_scr.at[pl.ds(n * tiles_src, tiles_src)], sems.at[n])
            for n, src in enumerate((near_ref, far_ref))
        ]
        for copy in copies:
            copy.start()
        for copy in copies:
            copy.wait()

    count = counts_ref[unit]
    m_scr[...] = jnp.full_like(m_scr, LOW)
    l_scr[...] = jnp.zeros_like(l_scr)
    acc_scr[...] = jnp.zeros_like(acc_scr)

    def step(first, size, masked):
        ids = [lists_ref[unit, first + n] for n in range(size)]
        scores = []
        for h in range(heads):
            k_block = jnp.concatenate([kv_scr[t, h] for t in ids], axis=0)
            scores.append(
                lax.dot_general(
                    k_block, q_ref[0, :, pl.ds(h * DH, DH)], (((1,), (1,)), ((), ())),
                    preferred_element_type=jnp.float32,
                )
            )
        if masked:
            slot = first + lax.broadcasted_iota(jnp.int32, (size * TILE, 1), 0) // TILE
            valid = slot < count
        for h in range(heads):
            score = jnp.where(valid, scores[h], LOW) if masked else scores[h]
            m_old = m_scr[h]
            peak = jnp.max(jnp.max(score.reshape(-1, 8, TILE), axis=0), axis=0, keepdims=True)
            m_new = jnp.maximum(m_old, peak)
            m_scr[h] = m_new
            expo = jnp.exp2((score - m_new[:1]) * SCALE)
            if masked:
                expo = jnp.where(valid, expo, 0.0)
            alpha = jnp.exp2((m_old - m_new) * SCALE)
            l_scr[h] = l_scr[h] * alpha + jnp.sum(expo.reshape(-1, 8, TILE), axis=0)
            v_block = jnp.concatenate([kv_scr[t, heads + h] for t in ids], axis=1)
            acc_scr[h] = acc_scr[h] * alpha[:1] + jnp.dot(
                v_block, expo.astype(jnp.bfloat16), preferred_element_type=jnp.float32
            )

    full = count // STEP
    rest = count - full * STEP

    def loop_body(i, carry):
        step(i * STEP, STEP, False)
        return carry

    lax.fori_loop(0, full, loop_body, 0)

    @pl.when(rest > STEP // 2)
    def _():
        step(full * STEP, STEP, True)

    @pl.when((rest > 0) & (rest <= STEP // 2))
    def _():
        step(full * STEP, STEP // 2, True)

    for h in range(heads):
        total = jnp.sum(l_scr[h], axis=0, keepdims=True)
        some = total > 0.0
        safe = jnp.where(some, total, 1.0)
        o_ref[0, :, pl.ds(h * DH, DH)] = (acc_scr[h] * (1.0 / safe)).astype(o_ref.dtype).T
        st_ref[0, h : h + 1] = jnp.where(some, m_scr[h][:1] * SCALE + jnp.log2(safe), LOW)


def attend(lists, counts, q, kv_near, kv_far):
    units, rows, width = q.shape
    heads = width // DH
    as_tiles = lambda t: t.reshape(-1, 2 * heads, TILE, DH)
    kv_near, kv_far = as_tiles(kv_near), as_tiles(kv_far)
    tiles_src = kv_near.shape[0]
    anywhere = pl.BlockSpec(memory_space=pl.ANY)
    grid_spec = pltpu.PrefetchScalarGridSpec(
        num_scalar_prefetch=2,
        grid=(units,),
        in_specs=[pl.BlockSpec((1, rows, width), lambda u, *_: (u, 0, 0))] + [anywhere] * 2,
        out_specs=[
            pl.BlockSpec((1, rows, width), lambda u, *_: (u, 0, 0)),
            pl.BlockSpec((1, 8, TILE), lambda u, *_: (u, 0, 0)),
        ],
        scratch_shapes=[
            pltpu.VMEM((2 * tiles_src, 2 * heads, TILE, DH), jnp.bfloat16),
            pltpu.VMEM((heads, 8, TILE), jnp.float32),
            pltpu.VMEM((heads, 8, TILE), jnp.float32),
            pltpu.VMEM((heads, DH, TILE), jnp.float32),
            pltpu.SemaphoreType.DMA((2,)),
        ],
    )
    return pl.pallas_call(
        functools.partial(attend_kernel, heads, tiles_src),
        grid_spec=grid_spec,
        out_shape=[
            jax.ShapeDtypeStruct((units, rows, width), jnp.bfloat16),
            jax.ShapeDtypeStruct((units, 8, TILE), jnp.float32),
        ],
        name="attend",
    )(lists, counts, q, kv_near, kv_far)


def merge_kernel(heads, units, oa_ref, sa_ref, ob_ref, sb_ref, o_ref):
    for u in range(units):
        top = jnp.maximum(sa_ref[u], sb_ref[u])
        weight_a = jnp.exp2(sa_ref[u] - top)
        weight_b = jnp.exp2(sb_ref[u] - top)
        total = weight_a + weight_b
        weights = jnp.concatenate([weight_a / total, weight_b / total], axis=0)
        weights = jnp.concatenate([weights, jnp.zeros((TILE - 16, TILE), jnp.float32)], axis=0).T
        for h in range(heads):
            cols = pl.ds(h * DH, DH)
            merged = oa_ref[u, :, cols].astype(jnp.float32) * weights[:, h : h + 1]
            merged = merged + ob_ref[u, :, cols].astype(jnp.float32) * weights[:, 8 + h : 9 + h]
            o_ref[u, :, cols] = merged.astype(o_ref.dtype)


def merge(oa, sa, ob, sb):
    units, rows, width = oa.shape
    some = math.gcd(units, 4)
    o_spec = pl.BlockSpec((some, rows, width), lambda u: (u, 0, 0))
    s_spec = pl.BlockSpec((some, 8, TILE), lambda u: (u, 0, 0))
    return pl.pallas_call(
        functools.partial(merge_kernel, width // DH, some),
        grid=(units // some,),
        in_specs=[o_spec, s_spec, o_spec, s_spec],
        out_specs=o_spec,
        out_shape=jax.ShapeDtypeStruct(oa.shape, oa.dtype),
        name="merge",
    )(oa, sa, ob, sb)


def join_columns(blocks):
    parts = len(blocks)
    members, rows, width = blocks[0].shape

    def body(*refs):
        ins, o_ref, sems = refs[:parts], refs[parts], refs[parts + 1]
        copies = [
            pltpu.make_async_copy(ins[p].at[j], o_ref.at[:, pl.ds((j * parts + p) * width, width)], sems.at[p, j])
            for p in range(parts)
            for j in range(members)
        ]
        for copy in copies:
            copy.start()
        for copy in copies:
            copy.wait()

    anywhere = pl.BlockSpec(memory_space=pl.ANY)
    return pl.pallas_call(
        body,
        in_specs=[anywhere] * parts,
        out_specs=anywhere,
        scratch_shapes=[pltpu.SemaphoreType.DMA((parts, members))],
        out_shape=jax.ShapeDtypeStruct((rows, members * parts * width), blocks[0].dtype),
        name="join_columns",
    )(*blocks)


def key_lists(tile_list, span, group, kv_index, members):
    shard = tile_list // span
    owner = shard // 2
    inside = owner // members == group
    local = jnp.where(shard % 2 == kv_index, 0, members * span) + owner % members * span + tile_list % span
    slots = tile_list.shape[1]
    slot = jnp.arange(slots, dtype=jnp.int32)
    before = (slot[:, None] < slot[None, :]).astype(jnp.int32)
    flag = inside.astype(jnp.int32)
    place = jnp.sum(flag[:, :, None] * before[None], axis=1)
    hit = inside[:, :, None] & (place[:, :, None] == slot[None, None, :])
    packed = jnp.sum(jnp.where(hit, local[:, :, None], 0), axis=1)
    return packed, jnp.sum(flag, axis=1)


def local(queries, keys, values, tile_list):
    n_head = lax.axis_size("head")
    members = n_head // GROUPS
    parts = math.gcd(HEADS // members, 2)
    kv_index = lax.axis_index("kv")
    head_index = lax.axis_index("head")
    group = head_index // members
    groups = [list(range(g * members, (g + 1) * members)) for g in range(GROUPS)]
    across = [(i, (i + members) % n_head) for i in range(n_head)]
    swap = [(0, 1), (1, 0)]
    units_src = queries.shape[0] // 2 // TILE
    units = members * units_src

    exchange = functools.partial(
        lax.all_to_all, axis_name="head", split_axis=0, concat_axis=0, axis_index_groups=groups, tiled=True
    )
    then = lambda first, later: lax.optimization_barrier((first, later))

    packed, number = key_lists(tile_list, keys.shape[0] // TILE, group, kv_index, members)
    packed = packed.reshape(GROUPS, members, 2, units_src, -1)
    number = number.reshape(GROUPS, members, 2, units_src)

    def lists_of(g):
        pick = lambda t: lax.dynamic_index_in_dim(
            lax.dynamic_index_in_dim(t, g, 0, False), kv_index, 1, False
        )
        return pick(packed).reshape(units, -1), pick(number).reshape(-1)

    far_lists, near_lists = lists_of(1 - group), lists_of(group)

    as_units = lambda t: t.reshape(units, TILE, t.shape[2])
    q_blocks = split_queries(kv_index, queries, members, parts)
    kv_blocks = list(split_keys(keys, values, members, parts))

    q_near, q_far, kv = [], [], []
    for p in range(parts):
        q_block, kv_block = q_blocks[p], kv_blocks[p]
        if p:
            kv[p - 1], q_block = then(kv[p - 1], q_block)
        q_got = exchange(q_block)
        q_got, kv_block = then(q_got, kv_block)
        q_near.append(as_units(q_got))
        q_far.append(as_units(lax.ppermute(q_got, "head", across)))
        kv.append(exchange(kv_block))

    blocks = []
    for p in range(parts):
        kv_other = lax.ppermute(kv[p], "kv", swap)
        o_far, s_far = attend(*far_lists, q_far[p], kv[p], kv_other)
        o_back = lax.ppermute(o_far, "head", across)
        s_back = lax.ppermute(s_far, "head", across)
        o_near, s_near = attend(*near_lists, q_near[p], kv[p], kv_other)
        merged = merge(o_near, s_near, o_back, s_back)
        blocks.append(exchange(merged.reshape(members, -1, merged.shape[2])))
    return join_columns(blocks)


def solution(mesh):
    return jax.shard_map(
        local,
        mesh=mesh,
        in_specs=(
            P(("clip", "head"), None),
            P(("clip", "head", "kv"), None),
            P(("clip", "head", "kv"), None),
            P("clip", None),
        ),
        out_specs=P(("clip", "head", "kv"), None),
        check_vma=False,
    )
```

```python
import functools
import math

import jax
import jax.numpy as jnp
from jax import lax
from jax.experimental import pallas as pl
from jax.experimental.pallas import tpu as pltpu
from jax.sharding import PartitionSpec as P


HEADS = 32
DH = 128
TILE = 128
STEP = 8
GROUPS = 2
LOW = -1e30
SCALE = math.log2(math.e) / math.sqrt(DH)


def split_queries(kv_index, queries, members, parts):
    rows = queries.shape[0] // 2
    group = math.gcd(members, 4)
    width = queries.shape[1] // (members * parts)

    def body(c_ref, q_ref, *outs):
        for g in range(group):
            for p in range(parts):
                outs[p][g] = q_ref[:, pl.ds((g * parts + p) * width, width)]

    return pl.pallas_call(
        body,
        grid_spec=pltpu.PrefetchScalarGridSpec(
            num_scalar_prefetch=1,
            grid=(members // group,),
            in_specs=[pl.BlockSpec((rows, group * parts * width), lambda j, c: (c[0], j))],
            out_specs=[pl.BlockSpec((group, rows, width), lambda j, c: (j, 0, 0))] * parts,
        ),
        out_shape=[jax.ShapeDtypeStruct((members, rows, width), queries.dtype)] * parts,
        name="split_queries",
    )(kv_index.reshape(1), queries)


def split_keys(keys, values, members, parts):
    rows, features = keys.shape
    tiles = rows // TILE
    heads = features // DH // (members * parts)
    group = math.gcd(members, 2)
    width = features // members * group

    def body(k_ref, v_ref, *outs):
        for g in range(group):
            for p in range(parts):
                for h in range(heads):
                    cols = pl.ds(((g * parts + p) * heads + h) * DH, DH)
                    for t in range(tiles):
                        outs[p][g, t, h] = k_ref[pl.ds(t * TILE, TILE), cols]
                        outs[p][g, t, heads + h] = v_ref[pl.ds(t * TILE, TILE), cols].T

    block = pl.BlockSpec((rows, width), lambda j: (0, j))
    return pl.pallas_call(
        body,
        grid=(members // group,),
        in_specs=[block, block],
        out_specs=[pl.BlockSpec((group, tiles, 2 * heads, TILE, DH), lambda j: (j, 0, 0, 0, 0))] * parts,
        out_shape=[jax.ShapeDtypeStruct((members, tiles, 2 * heads, TILE, DH), keys.dtype)] * parts,
        name="split_keys",
    )(keys, values)


def attend_kernel(
    heads, tiles_src, lists_ref, counts_ref, q_ref, near_ref, far_ref, o_ref, st_ref,
    kv_scr, m_scr, l_scr, acc_scr, sems,
):
    unit = pl.program_id(0)

    @pl.when(unit == 0)
    def _():
        copies = [
            pltpu.make_async_copy(src, kv_scr.at[pl.ds(n * tiles_src, tiles_src)], sems.at[n])
            for n, src in enumerate((near_ref, far_ref))
        ]
        for copy in copies:
            copy.start()
        for copy in copies:
            copy.wait()

    count = counts_ref[unit]
    m_scr[...] = jnp.full_like(m_scr, LOW)
    l_scr[...] = jnp.zeros_like(l_scr)
    acc_scr[...] = jnp.zeros_like(acc_scr)

    def step(first, size, masked):
        ids = [lists_ref[unit, first + n] for n in range(size)]
        scores = []
        for h in range(heads):
            k_block = jnp.concatenate([kv_scr[t, h] for t in ids], axis=0)
            scores.append(
                lax.dot_general(
                    k_block, q_ref[0, :, pl.ds(h * DH, DH)], (((1,), (1,)), ((), ())),
                    preferred_element_type=jnp.float32,
                )
            )
        if masked:
            slot = first + lax.broadcasted_iota(jnp.int32, (size * TILE, 1), 0) // TILE
            valid = slot < count
        for h in range(heads):
            score = jnp.where(valid, scores[h], LOW) if masked else scores[h]
            m_old = m_scr[h]
            peak = jnp.max(jnp.max(score.reshape(-1, 8, TILE), axis=0), axis=0, keepdims=True)
            m_new = jnp.maximum(m_old, peak)
            m_scr[h] = m_new
            expo = jnp.exp2((score - m_new[:1]) * SCALE)
            if masked:
                expo = jnp.where(valid, expo, 0.0)
            alpha = jnp.exp2((m_old - m_new) * SCALE)
            l_scr[h] = l_scr[h] * alpha + jnp.sum(expo.reshape(-1, 8, TILE), axis=0)
            v_block = jnp.concatenate([kv_scr[t, heads + h] for t in ids], axis=1)
            acc_scr[h] = acc_scr[h] * alpha[:1] + jnp.dot(
                v_block, expo.astype(jnp.bfloat16), preferred_element_type=jnp.float32
            )

    full = count // STEP
    rest = count - full * STEP

    def loop_body(i, carry):
        step(i * STEP, STEP, False)
        return carry

    lax.fori_loop(0, full, loop_body, 0)

    @pl.when(rest > STEP // 2)
    def _():
        step(full * STEP, STEP, True)

    @pl.when((rest > 0) & (rest <= STEP // 2))
    def _():
        step(full * STEP, STEP // 2, True)

    for h in range(heads):
        total = jnp.sum(l_scr[h], axis=0, keepdims=True)
        some = total > 0.0
        safe = jnp.where(some, total, 1.0)
        o_ref[0, :, pl.ds(h * DH, DH)] = (acc_scr[h] * (1.0 / safe)).astype(o_ref.dtype).T
        st_ref[0, h : h + 1] = jnp.where(some, m_scr[h][:1] * SCALE + jnp.log2(safe), LOW)


def attend(lists, counts, q, kv_near, kv_far):
    units, rows, width = q.shape
    heads = width // DH
    as_tiles = lambda t: t.reshape(-1, 2 * heads, TILE, DH)
    kv_near, kv_far = as_tiles(kv_near), as_tiles(kv_far)
    tiles_src = kv_near.shape[0]
    anywhere = pl.BlockSpec(memory_space=pl.ANY)
    grid_spec = pltpu.PrefetchScalarGridSpec(
        num_scalar_prefetch=2,
        grid=(units,),
        in_specs=[pl.BlockSpec((1, rows, width), lambda u, *_: (u, 0, 0))] + [anywhere] * 2,
        out_specs=[
            pl.BlockSpec((1, rows, width), lambda u, *_: (u, 0, 0)),
            pl.BlockSpec((1, 8, TILE), lambda u, *_: (u, 0, 0)),
        ],
        scratch_shapes=[
            pltpu.VMEM((2 * tiles_src, 2 * heads, TILE, DH), jnp.bfloat16),
            pltpu.VMEM((heads, 8, TILE), jnp.float32),
            pltpu.VMEM((heads, 8, TILE), jnp.float32),
            pltpu.VMEM((heads, DH, TILE), jnp.float32),
            pltpu.SemaphoreType.DMA((2,)),
        ],
    )
    return pl.pallas_call(
        functools.partial(attend_kernel, heads, tiles_src),
        grid_spec=grid_spec,
        out_shape=[
            jax.ShapeDtypeStruct((units, rows, width), jnp.bfloat16),
            jax.ShapeDtypeStruct((units, 8, TILE), jnp.float32),
        ],
        name="attend",
    )(lists, counts, q, kv_near, kv_far)


def merge_kernel(heads, units, oa_ref, sa_ref, ob_ref, sb_ref, o_ref):
    for u in range(units):
        top = jnp.maximum(sa_ref[u], sb_ref[u])
        weight_a = jnp.exp2(sa_ref[u] - top)
        weight_b = jnp.exp2(sb_ref[u] - top)
        total = weight_a + weight_b
        weights = jnp.concatenate([weight_a / total, weight_b / total], axis=0)
        weights = jnp.concatenate([weights, jnp.zeros((TILE - 16, TILE), jnp.float32)], axis=0).T
        for h in range(heads):
            cols = pl.ds(h * DH, DH)
            merged = oa_ref[u, :, cols].astype(jnp.float32) * weights[:, h : h + 1]
            merged = merged + ob_ref[u, :, cols].astype(jnp.float32) * weights[:, 8 + h : 9 + h]
            o_ref[u, :, cols] = merged.astype(o_ref.dtype)


def merge(oa, sa, ob, sb):
    units, _, width = oa.shape
    near = pl.BlockSpec(memory_space=pltpu.VMEM)
    return pl.pallas_call(
        functools.partial(merge_kernel, width // DH, units),
        in_specs=[near] * 4,
        out_specs=near,
        out_shape=jax.ShapeDtypeStruct(oa.shape, oa.dtype),
        name="merge",
    )(oa, sa, ob, sb)


def join_columns(blocks):
    parts = len(blocks)
    members, rows, width = blocks[0].shape

    def body(*refs):
        o_ref = refs[parts]
        for j in range(members):
            for p in range(parts):
                o_ref[:, pl.ds((j * parts + p) * width, width)] = refs[p][j]

    near = pl.BlockSpec(memory_space=pltpu.VMEM)
    return pl.pallas_call(
        body,
        in_specs=[near] * parts,
        out_specs=near,
        out_shape=jax.ShapeDtypeStruct((rows, members * parts * width), blocks[0].dtype),
        name="join_columns",
    )(*blocks)


def key_lists(tile_list, span, group, kv_index, members):
    shard = tile_list // span
    owner = shard // 2
    inside = owner // members == group
    local = jnp.where(shard % 2 == kv_index, 0, members * span) + owner % members * span + tile_list % span
    slots = tile_list.shape[1]
    slot = jnp.arange(slots, dtype=jnp.int32)
    before = (slot[:, None] < slot[None, :]).astype(jnp.int32)
    flag = inside.astype(jnp.int32)
    place = jnp.sum(flag[:, :, None] * before[None], axis=1)
    hit = inside[:, :, None] & (place[:, :, None] == slot[None, None, :])
    packed = jnp.sum(jnp.where(hit, local[:, :, None], 0), axis=1)
    return packed, jnp.sum(flag, axis=1)


def local(queries, keys, values, tile_list):
    n_head = lax.axis_size("head")
    members = n_head // GROUPS
    parts = math.gcd(HEADS // members, 2)
    kv_index = lax.axis_index("kv")
    head_index = lax.axis_index("head")
    group = head_index // members
    groups = [list(range(g * members, (g + 1) * members)) for g in range(GROUPS)]
    across = [(i, (i + members) % n_head) for i in range(n_head)]
    swap = [(0, 1), (1, 0)]
    units_src = queries.shape[0] // 2 // TILE
    units = members * units_src

    exchange = functools.partial(
        lax.all_to_all, axis_name="head", split_axis=0, concat_axis=0, axis_index_groups=groups, tiled=True
    )
    then = lambda first, later: lax.optimization_barrier((first, later))

    packed, number = key_lists(tile_list, keys.shape[0] // TILE, group, kv_index, members)
    packed = packed.reshape(GROUPS, members, 2, units_src, -1)
    number = number.reshape(GROUPS, members, 2, units_src)

    def lists_of(g):
        pick = lambda t: lax.dynamic_index_in_dim(
            lax.dynamic_index_in_dim(t, g, 0, False), kv_index, 1, False
        )
        return pick(packed).reshape(units, -1), pick(number).reshape(-1)

    far_lists, near_lists = lists_of(1 - group), lists_of(group)

    as_units = lambda t: t.reshape(units, TILE, t.shape[2])
    q_blocks = split_queries(kv_index, queries, members, parts)
    kv_blocks = list(split_keys(keys, values, members, parts))

    q_near, q_far, kv = [], [], []
    for p in range(parts):
        q_block, kv_block = q_blocks[p], kv_blocks[p]
        if p:
            kv[p - 1], q_block = then(kv[p - 1], q_block)
        q_got = exchange(q_block)
        q_got, kv_block = then(q_got, kv_block)
        q_near.append(as_units(q_got))
        q_far.append(as_units(lax.ppermute(q_got, "head", across)))
        kv.append(exchange(kv_block))

    blocks = []
    for p in range(parts):
        kv_other = lax.ppermute(kv[p], "kv", swap)
        o_far, s_far = attend(*far_lists, q_far[p], kv[p], kv_other)
        o_back = lax.ppermute(o_far, "head", across)
        s_back = lax.ppermute(s_far, "head", across)
        o_near, s_near = attend(*near_lists, q_near[p], kv[p], kv_other)
        merged = merge(o_near, s_near, o_back, s_back)
        blocks.append(exchange(merged.reshape(members, -1, merged.shape[2])))
    return join_columns(blocks)


def solution(mesh):
    return jax.shard_map(
        local,
        mesh=mesh,
        in_specs=(
            P(("clip", "head"), None),
            P(("clip", "head", "kv"), None),
            P(("clip", "head", "kv"), None),
            P("clip", None),
        ),
        out_specs=P(("clip", "head", "kv"), None),
        check_vma=False,
    )
```

```python
import functools
import math

import jax
import jax.numpy as jnp
from jax import lax
from jax.experimental import pallas as pl
from jax.experimental.pallas import tpu as pltpu
from jax.sharding import PartitionSpec as P


HEADS = 32
DH = 128
TILE = 128
STEP = 6
GROUPS = 2
LOW = -1e30
SCALE = math.log2(math.e) / math.sqrt(DH)


def split_queries(kv_index, queries, members):
    rows = queries.shape[0] // 2
    group = math.gcd(members, 4)
    width = queries.shape[1] // members

    def body(c_ref, q_ref, o_ref):
        for g in range(group):
            o_ref[g] = q_ref[:, pl.ds(g * width, width)]

    return pl.pallas_call(
        body,
        grid_spec=pltpu.PrefetchScalarGridSpec(
            num_scalar_prefetch=1,
            grid=(members // group,),
            in_specs=[pl.BlockSpec((rows, group * width), lambda j, c: (c[0], j))],
            out_specs=pl.BlockSpec((group, rows, width), lambda j, c: (j, 0, 0)),
        ),
        out_shape=jax.ShapeDtypeStruct((members, rows, width), queries.dtype),
        name="split_queries",
    )(kv_index.reshape(1), queries)


def split_keys(keys, values, members, parts):
    rows, features = keys.shape
    tiles = rows // TILE
    heads = features // DH // (members * parts)
    group = math.gcd(members, 2)
    width = features // members * group

    def body(k_ref, v_ref, *outs):
        for g in range(group):
            for p in range(parts):
                for h in range(heads):
                    cols = pl.ds(((g * parts + p) * heads + h) * DH, DH)
                    for t in range(tiles):
                        outs[p][g, t, h] = k_ref[pl.ds(t * TILE, TILE), cols]
                        outs[p][g, t, heads + h] = v_ref[pl.ds(t * TILE, TILE), cols].T

    block = pl.BlockSpec((rows, width), lambda j: (0, j))
    return pl.pallas_call(
        body,
        grid=(members // group,),
        in_specs=[block, block],
        out_specs=[pl.BlockSpec((group, tiles, 2 * heads, TILE, DH), lambda j: (j, 0, 0, 0, 0))] * parts,
        out_shape=[jax.ShapeDtypeStruct((members, tiles, 2 * heads, TILE, DH), keys.dtype)] * parts,
        name="split_keys",
    )(keys, values)


def attend_kernel(
    heads, tiles_src, lists_ref, counts_ref, q_ref, near_ref, far_ref, o_ref, st_ref,
    kv_scr, s_scr, p_scr, peak_scr, m_scr, l_scr, alpha_scr, acc_scr, sems,
):
    units = q_ref.shape[0]
    blank = 2 * tiles_src
    copies = [
        pltpu.make_async_copy(src, kv_scr.at[pl.ds(n * tiles_src, tiles_src)], sems.at[n])
        for n, src in enumerate((near_ref, far_ref))
    ]
    for copy in copies:
        copy.start()
    kv_scr[blank] = jnp.zeros_like(kv_scr[blank])
    p_scr[...] = jnp.zeros_like(p_scr)
    m_scr[...] = jnp.full_like(m_scr, LOW)
    l_scr[...] = jnp.zeros_like(l_scr)
    alpha_scr[...] = jnp.zeros_like(alpha_scr)
    acc_scr[...] = jnp.zeros_like(acc_scr)
    for copy in copies:
        copy.wait()

    def score(unit, first):
        count = counts_ref[unit]
        ids = [lists_ref[unit, jnp.where(first + n < count, first + n, 0)] for n in range(STEP)]
        for h in range(heads):
            k_block = jnp.concatenate([kv_scr[t, h] for t in ids], axis=0)
            found = lax.dot_general(
                k_block, q_ref[unit, :, pl.ds(h * DH, DH)], (((1,), (1,)), ((), ())),
                preferred_element_type=jnp.float32,
            )
            s_scr[h] = found
            peak_scr[h] = jnp.max(found.reshape(-1, 8, TILE), axis=0)

    def weigh(unit, first):
        count = counts_ref[unit]
        for h in range(heads):
            m_old = jnp.where(first == 0, LOW, m_scr[h])
            m_new = jnp.maximum(m_old, jnp.max(peak_scr[h], axis=0, keepdims=True))
            alpha = jnp.exp2((m_old - m_new) * SCALE)
            m_scr[h] = m_new
            alpha_scr[h] = alpha
            total = l_scr[h] * alpha
            for n in range(STEP):
                rows = pl.ds(n * TILE, TILE)
                expo = jnp.exp2((s_scr[h, rows] - m_new[:1]) * SCALE)
                p_scr[h, rows] = expo.astype(jnp.bfloat16)
                part = jnp.sum(expo.reshape(-1, 8, TILE), axis=0)
                total = total + jnp.where(first + n < count, part, 0.0)
            l_scr[h] = total

    def gather(unit, first):
        count = counts_ref[unit]
        ids = [jnp.where(first + n < count, lists_ref[unit, jnp.minimum(first + n, lists_ref.shape[1] - 1)], blank)
               for n in range(STEP)]
        for h in range(heads):
            v_block = jnp.concatenate([kv_scr[t, heads + h] for t in ids], axis=1)
            acc = acc_scr[h] * alpha_scr[h, :1] + jnp.dot(v_block, p_scr[h], preferred_element_type=jnp.float32)
            acc_scr[h] = acc
            total = jnp.sum(l_scr[h], axis=0, keepdims=True)
            some = total > 0.0
            safe = jnp.where(some, total, 1.0)
            o_ref[unit, :, pl.ds(h * DH, DH)] = (acc * (1.0 / safe)).astype(o_ref.dtype).T
            st_ref[unit, h : h + 1] = jnp.where(some, m_scr[h, :1] * SCALE + jnp.log2(safe), LOW)

    zero = jnp.int32(0)
    steps = lax.fori_loop(
        0, units, lambda u, n: n + jnp.maximum((counts_ref[u] + (STEP - 1)) // STEP, 1), zero
    )

    def following(unit, first):
        more = first + STEP < counts_ref[unit]
        return (
            jnp.where(more, unit, jnp.minimum(unit + 1, units - 1)),
            jnp.where(more, first + STEP, 0),
        )

    def body(i, carry):
        before, now = carry
        later = following(*now)
        gather(*before)
        weigh(*now)
        score(*later)
        return now, later

    score(zero, zero)
    last, _ = lax.fori_loop(0, steps, body, ((zero, zero), (zero, zero)))
    gather(*last)


def attend(lists, counts, q, kv_near, kv_far):
    units, rows, width = q.shape
    heads = width // DH
    as_tiles = lambda t: t.reshape(-1, 2 * heads, TILE, DH)
    kv_near, kv_far = as_tiles(kv_near), as_tiles(kv_far)
    tiles_src = kv_near.shape[0]
    anywhere = pl.BlockSpec(memory_space=pl.ANY)
    near = pl.BlockSpec(memory_space=pltpu.VMEM)
    scalars = pl.BlockSpec(memory_space=pltpu.SMEM)
    return pl.pallas_call(
        functools.partial(attend_kernel, heads, tiles_src),
        in_specs=[scalars, scalars, near, anywhere, anywhere],
        out_specs=[near, near],
        scratch_shapes=[
            pltpu.VMEM((2 * tiles_src + 1, 2 * heads, TILE, DH), jnp.bfloat16),
            pltpu.VMEM((heads, STEP * TILE, TILE), jnp.float32),
            pltpu.VMEM((heads, STEP * TILE, TILE), jnp.bfloat16),
            pltpu.VMEM((heads, 8, TILE), jnp.float32),
            pltpu.VMEM((heads, 8, TILE), jnp.float32),
            pltpu.VMEM((heads, 8, TILE), jnp.float32),
            pltpu.VMEM((heads, 8, TILE), jnp.float32),
            pltpu.VMEM((heads, DH, TILE), jnp.float32),
            pltpu.SemaphoreType.DMA((2,)),
        ],
        out_shape=[
            jax.ShapeDtypeStruct((units, rows, width), jnp.bfloat16),
            jax.ShapeDtypeStruct((units, 8, TILE), jnp.float32),
        ],
        name="attend",
    )(lists, counts, q, kv_near, kv_far)


def merge_kernel(heads, units, oa_ref, sa_ref, ob_ref, sb_ref, o_ref):
    for u in range(units):
        top = jnp.maximum(sa_ref[u], sb_ref[u])
        weight_a = jnp.exp2(sa_ref[u] - top)
        weight_b = jnp.exp2(sb_ref[u] - top)
        total = weight_a + weight_b
        weights = jnp.concatenate([weight_a / total, weight_b / total], axis=0)
        weights = jnp.concatenate([weights, jnp.zeros((TILE - 16, TILE), jnp.float32)], axis=0).T
        for h in range(heads):
            cols = pl.ds(h * DH, DH)
            merged = oa_ref[u, :, cols].astype(jnp.float32) * weights[:, h : h + 1]
            merged = merged + ob_ref[u, :, cols].astype(jnp.float32) * weights[:, 8 + h : 9 + h]
            o_ref[u, :, cols] = merged.astype(o_ref.dtype)


def merge(oa, sa, ob, sb):
    units, _, width = oa.shape
    near = pl.BlockSpec(memory_space=pltpu.VMEM)
    return pl.pallas_call(
        functools.partial(merge_kernel, width // DH, units),
        in_specs=[near] * 4,
        out_specs=near,
        out_shape=jax.ShapeDtypeStruct(oa.shape, oa.dtype),
        name="merge",
    )(oa, sa, ob, sb)


def join_columns(blocks):
    parts = len(blocks)
    members, rows, width = blocks[0].shape

    def body(*refs):
        o_ref = refs[parts]
        for j in range(members):
            for p in range(parts):
                o_ref[:, pl.ds((j * parts + p) * width, width)] = refs[p][j]

    near = pl.BlockSpec(memory_space=pltpu.VMEM)
    return pl.pallas_call(
        body,
        in_specs=[near] * parts,
        out_specs=near,
        out_shape=jax.ShapeDtypeStruct((rows, members * parts * width), blocks[0].dtype),
        name="join_columns",
    )(*blocks)


def key_lists(tile_list, span, group, kv_index, members):
    shard = tile_list // span
    owner = shard // 2
    inside = owner // members == group
    local = jnp.where(shard % 2 == kv_index, 0, members * span) + owner % members * span + tile_list % span
    slots = tile_list.shape[1]
    slot = jnp.arange(slots, dtype=jnp.int32)
    before = (slot[:, None] < slot[None, :]).astype(jnp.int32)
    flag = inside.astype(jnp.int32)
    place = jnp.sum(flag[:, :, None] * before[None], axis=1)
    hit = inside[:, :, None] & (place[:, :, None] == slot[None, None, :])
    packed = jnp.sum(jnp.where(hit, local[:, :, None], 0), axis=1)
    return packed, jnp.sum(flag, axis=1)


def local(queries, keys, values, tile_list):
    n_head = lax.axis_size("head")
    members = n_head // GROUPS
    parts = math.gcd(HEADS // members, 2)
    kv_index = lax.axis_index("kv")
    head_index = lax.axis_index("head")
    group = head_index // members
    groups = [list(range(g * members, (g + 1) * members)) for g in range(GROUPS)]
    across = [(i, (i + members) % n_head) for i in range(n_head)]
    swap = [(0, 1), (1, 0)]
    units_src = queries.shape[0] // 2 // TILE
    units = members * units_src

    exchange = functools.partial(
        lax.all_to_all, axis_name="head", split_axis=0, concat_axis=0, axis_index_groups=groups, tiled=True
    )
    then = lambda first, later: lax.optimization_barrier((first, later))

    packed, number = key_lists(tile_list, keys.shape[0] // TILE, group, kv_index, members)
    packed = packed.reshape(GROUPS, members, 2, units_src, -1)
    number = number.reshape(GROUPS, members, 2, units_src)

    def lists_of(g):
        pick = lambda t: lax.dynamic_index_in_dim(
            lax.dynamic_index_in_dim(t, g, 0, False), kv_index, 1, False
        )
        return pick(packed).reshape(units, -1), pick(number).reshape(-1)

    far_lists, near_lists = lists_of(1 - group), lists_of(group)

    q_blocks = split_queries(kv_index, queries, members)
    (far_lists, near_lists), keys = then((far_lists, near_lists), keys)
    kv_blocks = split_keys(keys, values, members, parts)
    q_got = exchange(q_blocks)
    q_got, kv_blocks = then(q_got, list(kv_blocks))
    q_units = q_got.reshape(units, TILE, -1)
    width = q_units.shape[2] // parts

    q_near, q_far, kv = [], [], []
    for p in range(parts):
        q_near.append(q_units[:, :, p * width : (p + 1) * width])
        q_far.append(lax.ppermute(q_near[p], "head", across))
        kv_block = kv_blocks[p]
        if p:
            kv[p - 1], kv_block = then(kv[p - 1], kv_block)
        kv.append(exchange(kv_block))

    blocks = []
    for p in range(parts):
        kv_other = lax.ppermute(kv[p], "kv", swap)
        o_far, s_far = attend(*far_lists, q_far[p], kv[p], kv_other)
        o_back = lax.ppermute(o_far, "head", across)
        s_back = lax.ppermute(s_far, "head", across)
        o_near, s_near = attend(*near_lists, q_near[p], kv[p], kv_other)
        merged = merge(o_near, s_near, o_back, s_back)
        blocks.append(exchange(merged.reshape(members, -1, merged.shape[2])))
    return join_columns(blocks)


def solution(mesh):
    return jax.shard_map(
        local,
        mesh=mesh,
        in_specs=(
            P(("clip", "head"), None),
            P(("clip", "head", "kv"), None),
            P(("clip", "head", "kv"), None),
            P("clip", None),
        ),
        out_specs=P(("clip", "head", "kv"), None),
        check_vma=False,
    )
```

```python
import functools
import math

import jax
import jax.numpy as jnp
from jax import lax
from jax.experimental import pallas as pl
from jax.experimental.pallas import tpu as pltpu
from jax.sharding import PartitionSpec as P


HEADS = 32
DH = 128
TILE = 128
STEP = 7
GROUPS = 2
LOW = -1e30
SCALE = math.log2(math.e) / math.sqrt(DH)


def split_queries(kv_index, queries, members):
    rows = queries.shape[0] // 2
    group = math.gcd(members, 4)
    width = queries.shape[1] // members

    def body(c_ref, q_ref, o_ref):
        for g in range(group):
            o_ref[g] = q_ref[:, pl.ds(g * width, width)]

    return pl.pallas_call(
        body,
        grid_spec=pltpu.PrefetchScalarGridSpec(
            num_scalar_prefetch=1,
            grid=(members // group,),
            in_specs=[pl.BlockSpec((rows, group * width), lambda j, c: (c[0], j))],
            out_specs=pl.BlockSpec((group, rows, width), lambda j, c: (j, 0, 0)),
        ),
        out_shape=jax.ShapeDtypeStruct((members, rows, width), queries.dtype),
        name="split_queries",
    )(kv_index.reshape(1), queries)


def split_keys(keys, values, members, parts):
    rows, features = keys.shape
    tiles = rows // TILE
    heads = features // DH // (members * parts)
    group = math.gcd(members, 2)
    width = features // members * group

    def body(k_ref, v_ref, *outs):
        for g in range(group):
            for p in range(parts):
                for h in range(heads):
                    cols = pl.ds(((g * parts + p) * heads + h) * DH, DH)
                    for t in range(tiles):
                        outs[p][g, t, h] = k_ref[pl.ds(t * TILE, TILE), cols]
                        outs[p][g, t, heads + h] = v_ref[pl.ds(t * TILE, TILE), cols].T

    block = pl.BlockSpec((rows, width), lambda j: (0, j))
    return pl.pallas_call(
        body,
        grid=(members // group,),
        in_specs=[block, block],
        out_specs=[pl.BlockSpec((group, tiles, 2 * heads, TILE, DH), lambda j: (j, 0, 0, 0, 0))] * parts,
        out_shape=[jax.ShapeDtypeStruct((members, tiles, 2 * heads, TILE, DH), keys.dtype)] * parts,
        name="split_keys",
    )(keys, values)


def attend_kernel(
    heads, tiles_src, sets, lists_ref, counts_ref, near_ref, far_ref, *rest
):
    q_srcs, o_dsts, st_dsts = rest[:sets], rest[sets : 2 * sets], rest[2 * sets : 3 * sets]
    q_ref, o_ref, st_ref, kv_scr, s_scr, p_scr, peak_scr, m_scr, l_scr, alpha_scr, acc_scr, sems = rest[3 * sets :]
    units = q_ref.shape[0]
    units_set = units // sets
    blank = 2 * tiles_src
    copies = [
        pltpu.make_async_copy(src, kv_scr.at[pl.ds(n * tiles_src, tiles_src)], sems.at[n])
        for n, src in enumerate((near_ref, far_ref))
    ]
    copies += [
        pltpu.make_async_copy(src, q_ref.at[pl.ds(n * units_set, units_set)], sems.at[2 + n])
        for n, src in enumerate(q_srcs)
    ]
    for copy in copies:
        copy.start()
    kv_scr[blank] = jnp.zeros_like(kv_scr[blank])
    p_scr[...] = jnp.zeros_like(p_scr)
    m_scr[...] = jnp.full_like(m_scr, LOW)
    l_scr[...] = jnp.zeros_like(l_scr)
    alpha_scr[...] = jnp.zeros_like(alpha_scr)
    acc_scr[...] = jnp.zeros_like(acc_scr)
    for copy in copies:
        copy.wait()

    def score(unit, first):
        count = counts_ref[unit]
        ids = [lists_ref[unit, jnp.where(first + n < count, first + n, 0)] for n in range(STEP)]
        for h in range(heads):
            k_block = jnp.concatenate([kv_scr[t, h] for t in ids], axis=0)
            found = lax.dot_general(
                k_block, q_ref[unit, :, pl.ds(h * DH, DH)], (((1,), (1,)), ((), ())),
                preferred_element_type=jnp.float32,
            )
            s_scr[h] = found
            peak_scr[h] = jnp.max(found.reshape(-1, 8, TILE), axis=0)

    def weigh(unit, first):
        count = counts_ref[unit]
        for h in range(heads):
            m_old = jnp.where(first == 0, LOW, m_scr[h])
            m_new = jnp.maximum(m_old, jnp.max(peak_scr[h], axis=0, keepdims=True))
            alpha = jnp.exp2((m_old - m_new) * SCALE)
            m_scr[h] = m_new
            alpha_scr[h] = alpha
            total = l_scr[h] * alpha
            for n in range(STEP):
                rows = pl.ds(n * TILE, TILE)
                expo = jnp.exp2((s_scr[h, rows] - m_new[:1]) * SCALE)
                p_scr[h, rows] = expo.astype(jnp.bfloat16)
                part = jnp.sum(expo.reshape(-1, 8, TILE), axis=0)
                total = total + jnp.where(first + n < count, part, 0.0)
            l_scr[h] = total

    def gather(unit, first):
        count = counts_ref[unit]
        ids = [jnp.where(first + n < count, lists_ref[unit, jnp.minimum(first + n, lists_ref.shape[1] - 1)], blank)
               for n in range(STEP)]
        for h in range(heads):
            v_block = jnp.concatenate([kv_scr[t, heads + h] for t in ids], axis=1)
            acc = acc_scr[h] * alpha_scr[h, :1] + jnp.dot(v_block, p_scr[h], preferred_element_type=jnp.float32)
            acc_scr[h] = acc
            total = jnp.sum(l_scr[h], axis=0, keepdims=True)
            some = total > 0.0
            safe = jnp.where(some, total, 1.0)
            o_ref[unit, :, pl.ds(h * DH, DH)] = (acc * (1.0 / safe)).astype(o_ref.dtype).T
            st_ref[unit, h : h + 1] = jnp.where(some, m_scr[h, :1] * SCALE + jnp.log2(safe), LOW)

    zero = jnp.int32(0)
    steps = lax.fori_loop(
        0, units, lambda u, n: n + jnp.maximum((counts_ref[u] + (STEP - 1)) // STEP, 1), zero
    )

    def following(unit, first):
        more = first + STEP < counts_ref[unit]
        return (
            jnp.where(more, unit, jnp.minimum(unit + 1, units - 1)),
            jnp.where(more, first + STEP, 0),
        )

    def body(i, carry):
        before, now = carry
        later = following(*now)
        gather(*before)
        weigh(*now)
        score(*later)
        return now, later

    score(zero, zero)
    last, _ = lax.fori_loop(0, steps, body, ((zero, zero), (zero, zero)))
    gather(*last)
    copies = []
    for n in range(sets):
        part = pl.ds(n * units_set, units_set)
        copies.append(pltpu.make_async_copy(o_ref.at[part], o_dsts[n], sems.at[n]))
        copies.append(pltpu.make_async_copy(st_ref.at[part], st_dsts[n], sems.at[sets + n]))
    for copy in copies:
        copy.start()
    for copy in copies:
        copy.wait()


def attend(lists, queries, kv_near, kv_far):
    sets = len(queries)
    packed = jnp.concatenate([packed for packed, _ in lists], axis=0)
    counts = jnp.concatenate([number for _, number in lists], axis=0)
    units, rows, width = queries[0].shape
    heads = width // DH
    as_tiles = lambda t: t.reshape(-1, 2 * heads, TILE, DH)
    kv_near, kv_far = as_tiles(kv_near), as_tiles(kv_far)
    tiles_src = kv_near.shape[0]
    anywhere = pl.BlockSpec(memory_space=pl.ANY)
    scalars = pl.BlockSpec(memory_space=pltpu.SMEM)
    found = pl.pallas_call(
        functools.partial(attend_kernel, heads, tiles_src, sets),
        in_specs=[scalars, scalars] + [anywhere] * (2 + sets),
        out_specs=[anywhere] * (2 * sets),
        scratch_shapes=[
            pltpu.VMEM((sets * units, rows, width), jnp.bfloat16),
            pltpu.VMEM((sets * units, rows, width), jnp.bfloat16),
            pltpu.VMEM((sets * units, 8, TILE), jnp.float32),
            pltpu.VMEM((2 * tiles_src + 1, 2 * heads, TILE, DH), jnp.bfloat16),
            pltpu.VMEM((heads, STEP * TILE, TILE), jnp.float32),
            pltpu.VMEM((heads, STEP * TILE, TILE), jnp.bfloat16),
            pltpu.VMEM((heads, 8, TILE), jnp.float32),
            pltpu.VMEM((heads, 8, TILE), jnp.float32),
            pltpu.VMEM((heads, 8, TILE), jnp.float32),
            pltpu.VMEM((heads, 8, TILE), jnp.float32),
            pltpu.VMEM((heads, DH, TILE), jnp.float32),
            pltpu.SemaphoreType.DMA((2 + 2 * sets,)),
        ],
        out_shape=[jax.ShapeDtypeStruct((units, rows, width), jnp.bfloat16)] * sets
        + [jax.ShapeDtypeStruct((units, 8, TILE), jnp.float32)] * sets,
        name="attend",
    )(packed, counts, kv_near, kv_far, *queries)
    return found[:sets], found[sets:]


def passed_on(numbers):
    def body(x_ref, o_ref):
        o_ref[...] = x_ref[...]

    near = pl.BlockSpec(memory_space=pltpu.VMEM)
    return pl.pallas_call(
        body,
        in_specs=[near],
        out_specs=near,
        out_shape=jax.ShapeDtypeStruct(numbers.shape, numbers.dtype),
        name="passed_on",
    )(numbers)


def merge_kernel(heads, units, oa_ref, sa_ref, ob_ref, sb_ref, o_ref):
    for u in range(units):
        top = jnp.maximum(sa_ref[u], sb_ref[u])
        weight_a = jnp.exp2(sa_ref[u] - top)
        weight_b = jnp.exp2(sb_ref[u] - top)
        total = weight_a + weight_b
        weights = jnp.concatenate([weight_a / total, weight_b / total], axis=0)
        weights = jnp.concatenate([weights, jnp.zeros((TILE - 16, TILE), jnp.float32)], axis=0).T
        for h in range(heads):
            cols = pl.ds(h * DH, DH)
            merged = oa_ref[u, :, cols].astype(jnp.float32) * weights[:, h : h + 1]
            merged = merged + ob_ref[u, :, cols].astype(jnp.float32) * weights[:, 8 + h : 9 + h]
            o_ref[u, :, cols] = merged.astype(o_ref.dtype)


def merge(oa, sa, ob, sb):
    units, _, width = oa.shape
    near = pl.BlockSpec(memory_space=pltpu.VMEM)
    return pl.pallas_call(
        functools.partial(merge_kernel, width // DH, units),
        in_specs=[near] * 4,
        out_specs=near,
        out_shape=jax.ShapeDtypeStruct(oa.shape, oa.dtype),
        name="merge",
    )(oa, sa, ob, sb)


def join_columns(blocks):
    parts = len(blocks)
    members, rows, width = blocks[0].shape

    def body(*refs):
        o_ref = refs[parts]
        for j in range(members):
            for p in range(parts):
                o_ref[:, pl.ds((j * parts + p) * width, width)] = refs[p][j]

    near = pl.BlockSpec(memory_space=pltpu.VMEM)
    return pl.pallas_call(
        body,
        in_specs=[near] * parts,
        out_specs=near,
        out_shape=jax.ShapeDtypeStruct((rows, members * parts * width), blocks[0].dtype),
        name="join_columns",
    )(*blocks)


def key_lists(tile_list, span, group, kv_index, members):
    shard = tile_list // span
    owner = shard // 2
    inside = owner // members == group
    local = jnp.where(shard % 2 == kv_index, 0, members * span) + owner % members * span + tile_list % span
    slots = tile_list.shape[1]
    slot = jnp.arange(slots, dtype=jnp.int32)
    before = (slot[:, None] < slot[None, :]).astype(jnp.int32)
    flag = inside.astype(jnp.int32)
    place = jnp.sum(flag[:, :, None] * before[None], axis=1)
    hit = inside[:, :, None] & (place[:, :, None] == slot[None, None, :])
    packed = jnp.sum(jnp.where(hit, local[:, :, None], 0), axis=1)
    return packed, jnp.sum(flag, axis=1)


def local(queries, keys, values, tile_list):
    n_head = lax.axis_size("head")
    members = n_head // GROUPS
    parts = math.gcd(HEADS // members, 2)
    kv_index = lax.axis_index("kv")
    head_index = lax.axis_index("head")
    group = head_index // members
    groups = [list(range(g * members, (g + 1) * members)) for g in range(GROUPS)]
    across = [(i, (i + members) % n_head) for i in range(n_head)]
    swap = [(0, 1), (1, 0)]
    units_src = queries.shape[0] // 2 // TILE
    units = members * units_src

    exchange = functools.partial(
        lax.all_to_all, axis_name="head", split_axis=0, concat_axis=0, axis_index_groups=groups, tiled=True
    )
    then = lambda first, later: lax.optimization_barrier((first, later))

    packed, number = key_lists(tile_list, keys.shape[0] // TILE, group, kv_index, members)
    packed = packed.reshape(GROUPS, members, 2, units_src, -1)
    number = number.reshape(GROUPS, members, 2, units_src)

    def lists_of(g):
        pick = lambda t: lax.dynamic_index_in_dim(
            lax.dynamic_index_in_dim(t, g, 0, False), kv_index, 1, False
        )
        return pick(packed).reshape(units, -1), pick(number).reshape(-1)

    far_lists, near_lists = lists_of(1 - group), lists_of(group)

    q_blocks = split_queries(kv_index, queries, members)
    (far_lists, near_lists), keys = then((far_lists, near_lists), keys)
    kv_blocks = split_keys(keys, values, members, parts)
    q_got = exchange(q_blocks)
    q_got, kv_blocks = then(q_got, list(kv_blocks))
    q_units = q_got.reshape(units, TILE, -1)
    width = q_units.shape[2] // parts

    q_near, q_far, kv = [], [], []
    for p in range(parts):
        q_near.append(q_units[:, :, p * width : (p + 1) * width])
        q_far.append(lax.ppermute(q_near[p], "head", across))
        kv_block = kv_blocks[p]
        if p:
            kv[p - 1], kv_block = then(kv[p - 1], kv_block)
        kv.append(exchange(kv_block))

    blocks = []
    for p in range(parts):
        kv_other = lax.ppermute(kv[p], "kv", swap)
        if p + 1 < parts:
            (o_near, o_far), (s_near, s_far) = attend((near_lists, far_lists), (q_near[p], q_far[p]), kv[p], kv_other)
        else:
            (o_far,), (s_far,) = attend((far_lists,), (q_far[p],), kv[p], kv_other)
            near_lists = passed_on(near_lists[0]), near_lists[1]
            (o_near,), (s_near,) = attend((near_lists,), (q_near[p],), kv[p], kv_other)
        o_back = lax.ppermute(o_far, "head", across)
        s_back = lax.ppermute(s_far, "head", across)
        merged = merge(o_near, s_near, o_back, s_back)
        blocks.append(exchange(merged.reshape(members, -1, merged.shape[2])))
    return join_columns(blocks)


def solution(mesh):
    return jax.shard_map(
        local,
        mesh=mesh,
        in_specs=(
            P(("clip", "head"), None),
            P(("clip", "head", "kv"), None),
            P(("clip", "head", "kv"), None),
            P("clip", None),
        ),
        out_specs=P(("clip", "head", "kv"), None),
        check_vma=False,
    )
```
